32 devices in a mesh: grp: 2 (over core), seq: 4 (over z), tp: 4 (over y, x).
Axes of the slice: x: 2, y: 2, z: 4, core: 2. Of those that a mesh axis runs over, the one named last changes fastest.
Arguments:
- patches_in: bfloat16 [8192, 1280], P(('grp', 'seq')), may hold values from -6 to 6
- gain_attn: float32 [1280], replicated, may hold values from 0.25 to 1.75
- gain_merge: float32 [1280], replicated, may hold values from 0.25 to 1.75
- qkv_weight: bfloat16 [1280, 3840], P(None, 'tp'), may hold values from -0.15625 to 0.15625
- out_weight: bfloat16 [1280, 1280], P('tp'), may hold values from -0.15625 to 0.15625
- cotangent: bfloat16 [2048, 5120], P(('grp', 'seq'), 'tp'), may hold values from -0.29882812 to 0.29882812
- patch_counts: int32 [32], P(('grp', 'seq')), may hold values from 64 to 256, as said below
- block_target: int32 [1024], P(('grp', 'seq')), may hold values from 0 to 1023, as said below
Outputs:
- image_rows: bfloat16 [2048, 5120], P(('grp', 'seq'), 'tp')
- grad_qkv: float32 [1280, 3840], P(('grp', 'seq'), 'tp')
- grad_out: float32 [1280, 1280], P('tp', ('grp', 'seq'))
The draws below stay inside these ranges and needn't reach their ends.
Inputs may be any that keep to these rules, and one draw needn't show every extreme that they name: `patch_counts`: multiples of 4; some image has 256 patches in every draw. `block_target`: each sequence block is named exactly once; the 128 blocks of one owner name exactly 16 blocks of each sequence shard (shard = value // 128).
All inputs are finite; a program needn't handle non-finite values.
Results may differ from the reference program's by a relative error of at most 0.02.
Values may be sent and summed in bfloat16 or wider, within the bound.
No kernel may reach another device: no remote copies, remote signals or barrier semaphores. Data moves between devices by JAX's collectives and lax.ppermute only.
A program may use at most 128 MiB of HBM per device.

```python
import jax
import jax.numpy as jnp
from jax import lax

DV = 1280
HEAD_V = 80
PATCH_MAX = 256
BROWS = 2
OWNERS = 8
IMAGES = 32
PATCHES = 8192
BLK_DEV = 128
CAPB = 16
BLOCKS = 1024
SEQ_ROWS = 2048


def draw_patch_counts(key, part):
    first_key, second_key = jax.random.split(jax.random.fold_in(key, 11))
    base = jax.random.randint(first_key, (IMAGES,), PATCH_MAX // 16, PATCH_MAX // 4 + 1) * 4
    chosen = jax.random.randint(second_key, (), 0, IMAGES)
    return jnp.where(jnp.arange(IMAGES) == chosen, PATCH_MAX, base).astype(jnp.int32)


def draw_block_target(key, part):
    first_key, second_key = jax.random.split(jax.random.fold_in(key, 23))
    sender_perm = jax.vmap(lambda inner: jax.random.permutation(inner, BLK_DEV))(jax.random.split(first_key, OWNERS))
    shard = sender_perm // CAPB
    within = sender_perm % CAPB
    shard_perm = jax.vmap(lambda inner: jax.random.permutation(inner, BLK_DEV))(jax.random.split(second_key, OWNERS))
    arrival = jnp.arange(OWNERS)[:, None] * CAPB + within
    slot_ids = shard_perm[shard, arrival]
    return (shard * BLK_DEV + slot_ids).reshape(BLOCKS).astype(jnp.int32)


def levels(key, dims, cuts, low, high):
    def one(position, parts):
        heights = jax.random.uniform(jax.random.fold_in(jax.random.fold_in(key, 6), position), (parts,), jnp.float32, low / len(cuts), high / len(cuts))
        return jnp.repeat(jnp.exp(heights), dims[position] // parts).reshape((-1,) + (1,) * (len(dims) - position - 1))

    level = one(*cuts[0])
    for cut in cuts[1:]:
        level = level * one(*cut)
    return level


def bell_draw(key, extent, width, reach, cuts=(), kind=jnp.bfloat16):
    array = width * jax.random.normal(key, extent, jnp.float32)
    if cuts:
        array = array * levels(key, extent, cuts, -0.22, 0.18)
    return jnp.clip(array, -reach, reach).astype(kind)


def setup_inputs(seed: int = 0) -> dict:
    keys = jax.random.split(jax.random.key(seed), 9)
    return {
        "patches_in": bell_draw(keys[0], (PATCHES, DV), 1.0, 6.0, ((0, 8),)),
        "gain_attn": jnp.clip(1.0 + 0.15 * jax.random.normal(keys[1], (DV,), jnp.float32), 0.25, 1.75),
        "gain_merge": jnp.clip(1.0 + 0.15 * jax.random.normal(keys[2], (DV,), jnp.float32), 0.25, 1.75),
        "qkv_weight": bell_draw(keys[3], (DV, 3 * DV), DV ** -0.5, 0.15625, ((1, 4),)),
        "out_weight": bell_draw(keys[4], (DV, DV), DV ** -0.5, 0.15625, ((0, 4),)),
        "cotangent": bell_draw(keys[5], (SEQ_ROWS, 4 * DV), 0.05, 0.29882812, ((0, 8), (1, 4))),
        "patch_counts": draw_patch_counts(jax.random.fold_in(keys[8], 71), 0),
        "block_target": draw_block_target(jax.random.fold_in(keys[8], 71), 0),
    }


def layer_norm(values, gain):
    center = values - lax.optimization_barrier(jnp.mean(values, axis=-1, keepdims=True))
    spread = lax.optimization_barrier(jnp.mean(center * center, axis=-1, keepdims=True))
    return center * lax.rsqrt(spread + 1e-06) * gain.astype(jnp.float32)

def attend(qkv_rows, count):
    length = qkv_rows.shape[0]
    heads_here = qkv_rows.shape[1] // (3 * HEAD_V)
    split_heads = qkv_rows.reshape(length, heads_here, 3, HEAD_V)
    queries = split_heads[:, :, 0]
    keys_all = split_heads[:, :, 1]
    values_all = split_heads[:, :, 2]
    scores = jnp.einsum('qhd,khd->hqk', queries, keys_all, preferred_element_type=jnp.float32) * HEAD_V ** (-0.5)
    key_live = jnp.arange(length) < count
    scores = jnp.where(key_live[None, None, :], scores, -1e+30)
    scores = scores - lax.optimization_barrier(jnp.max(scores, axis=-1, keepdims=True))
    weights = jnp.exp(scores)
    weights = (weights / lax.optimization_barrier(jnp.sum(weights, axis=-1, keepdims=True))).astype(jnp.bfloat16)
    mixed = jnp.einsum('hqk,khd->qhd', weights, values_all, preferred_element_type=jnp.float32)
    return mixed.reshape(length, heads_here * HEAD_V).astype(jnp.bfloat16)

def attend_back(qkv_rows, count, grad_heads):
    pull_back = jax.vjp(lambda inner: attend(inner, count), qkv_rows)[1]
    return pull_back(grad_heads)[0]

def reference(patches_in, gain_attn, gain_merge, qkv_weight, out_weight, cotangent, patch_counts, block_target):
    normed = layer_norm(patches_in.astype(jnp.float32), gain_attn).astype(jnp.bfloat16)
    qkv_rows = jnp.dot(normed, qkv_weight, preferred_element_type=jnp.float32).astype(jnp.bfloat16)
    per_image = qkv_rows.reshape(IMAGES, PATCH_MAX, 3 * DV)
    head_out = lax.map(lambda pair: attend(pair[0], pair[1]), (per_image, patch_counts)).reshape(PATCHES, DV)
    attn_sum = jnp.dot(head_out, out_weight, preferred_element_type=jnp.float32)
    residual = patches_in.astype(jnp.float32) + attn_sum
    live_rows = (jnp.arange(PATCH_MAX)[None, :] < patch_counts[:, None]).reshape(PATCHES, 1).astype(jnp.float32)

    def merge_norm(inner):
        return layer_norm(inner, gain_merge) * live_rows
    merged, pull_back = jax.vjp(merge_norm, residual)
    merged = merged.astype(jnp.bfloat16)
    blocks_all = merged.reshape(BLOCKS, BROWS, 4 * DV)
    image_rows = jnp.zeros_like(blocks_all).at[block_target].set(blocks_all).reshape(SEQ_ROWS, 4 * DV)
    incoming = cotangent.reshape(BLOCKS, BROWS, 4 * DV)[block_target].reshape(PATCHES, DV)
    grad_attn = pull_back(incoming.astype(jnp.float32))[0].astype(jnp.bfloat16)
    grad_out = jnp.dot(head_out.T, grad_attn, preferred_element_type=jnp.float32)
    grad_heads = jnp.dot(grad_attn, out_weight.T, preferred_element_type=jnp.float32).astype(jnp.bfloat16)
    grad_qkv_rows = lax.map(lambda trio: attend_back(trio[0], trio[1], trio[2]), (per_image, patch_counts, grad_heads.reshape(IMAGES, PATCH_MAX, DV)))
    grad_qkv = jnp.dot(normed.T, grad_qkv_rows.reshape(PATCHES, 3 * DV), preferred_element_type=jnp.float32)
    return (image_rows, grad_qkv, grad_out)
```

```python
import functools

import jax
import jax.numpy as jnp
from jax import lax
from jax.experimental import pallas as pl
from jax.experimental.pallas import tpu as pltpu
from jax.sharding import PartitionSpec as P

HEAD_V = 80
LANES = 128
F32 = jnp.float32
BF16 = jnp.bfloat16
NN = (((1,), (0,)), ((), ()))
NT = (((1,), (1,)), ((), ()))
TN = (((0,), (0,)), ((), ()))


def mm(a, b, dims=NN):
    return lax.dot_general(a, b, dims, preferred_element_type=F32)


def iota(shape, axis):
    return lax.broadcasted_iota(jnp.int32, shape, axis)


def swap(value, axes, step, size):
    return lax.ppermute(value, axes, [(i, i ^ step) for i in range(size)])


def whole(array):
    return pl.BlockSpec(array.shape, lambda *_, n=len(array.shape): (0,) * n)


def one_hot(test):
    return test.astype(F32).astype(BF16)


def folds(rows, cols):
    rest = cols % LANES
    if rest and LANES % rest == 0 and rows % (LANES // rest) == 0:
        return LANES // rest
    return 1


def packed_rows(rows, cols):
    rest = rows // folds(rows, cols) if cols % LANES else 0
    return cols // LANES * rows + rest


def pack(x):
    rows, cols = x.shape
    full, rest = cols // LANES * LANES, cols % LANES
    outs = [x[:, i : i + LANES] for i in range(0, full, LANES)]
    if rest:
        fold = folds(rows, cols)
        size = rows // fold
        tail = [x[i * size : (i + 1) * size, full:] for i in range(fold)]
        if fold * rest < LANES:
            tail.append(jnp.zeros((size, LANES - fold * rest), x.dtype))
        outs.append(jnp.concatenate(tail, axis=1))
    return jnp.concatenate(outs, axis=0)


def unpack(x, rows, cols):
    full, rest = cols // LANES * LANES, cols % LANES
    outs = [x[i * rows : (i + 1) * rows] for i in range(cols // LANES)]
    if rest:
        fold = folds(rows, cols)
        tail = x[cols // LANES * rows :]
        outs.append(jnp.concatenate([tail[:, i * rest : (i + 1) * rest] for i in range(fold)], axis=0))
    return jnp.concatenate(outs, axis=1)


def forward_kernel(n_tp, heads, first, ids, counts, x_ref, gain_ref, w_ref, own_ref, normed_ref, qkv_ref, *out_refs):
    image = pl.program_id(0)
    length = x_ref.shape[0]
    groups = length // n_tp
    row = iota((length, length), 0)
    source = (row % groups) * n_tp + ((row // groups) ^ ids[0])
    x = mm(one_hot(iota((length, length), 1) == source), x_ref[...])
    own_ref[...] = x[:groups].astype(BF16)
    center = x - jnp.mean(x, axis=-1, keepdims=True)
    spread = jnp.mean(center * center, axis=-1, keepdims=True)
    normed = (center * lax.rsqrt(spread + 1e-06) * gain_ref[...]).astype(BF16)
    normed_ref[...] = normed
    qkv = mm(normed, w_ref[...], NT).astype(BF16)
    live = (iota((1, length), 1) % groups) * n_tp < counts[first + image]
    outs = []
    for head in range(heads):
        part = qkv[:, head * 3 * HEAD_V : (head + 1) * 3 * HEAD_V]
        qkv_ref[head] = part
        scores = mm(part[:, :HEAD_V], part[:, HEAD_V : 2 * HEAD_V], NT) * HEAD_V ** (-0.5)
        scores = jnp.where(live, scores, -1e30)
        scores = jnp.exp(scores - jnp.max(scores, axis=-1, keepdims=True))
        probs = (scores * (1.0 / jnp.sum(scores, axis=-1, keepdims=True))).astype(BF16)
        outs.append(mm(probs, part[:, 2 * HEAD_V :]))
    out = jnp.concatenate(outs, axis=1)
    for step in range(n_tp):
        out_refs[step][...] = pack(out[step * groups : (step + 1) * groups]).astype(BF16)


def forward(ids, counts, x, gain, weight, n_tp, first, some):
    width = x.shape[1]
    length = x.shape[0] // counts.shape[0]
    rows = some * length
    groups = length // n_tp
    cols = weight.shape[0]
    heads = cols // (3 * HEAD_V)
    size = packed_rows(groups, heads * HEAD_V)
    return pl.pallas_call(
        functools.partial(forward_kernel, n_tp, heads, first),
        grid_spec=pltpu.PrefetchScalarGridSpec(
            num_scalar_prefetch=2,
            grid=(some,),
            in_specs=[
                pl.BlockSpec((length, width), lambda i, *_: (first + i, 0)),
                pl.BlockSpec((1, width), lambda i, *_: (0, 0)),
                pl.BlockSpec((cols, width), lambda i, *_: (0, 0)),
            ],
            out_specs=[
                pl.BlockSpec((groups, width), lambda i, *_: (i, 0)),
                pl.BlockSpec((length, width), lambda i, *_: (i, 0)),
                pl.BlockSpec((heads, length, 3 * HEAD_V), lambda i, *_: (0, i, 0)),
            ]
            + [pl.BlockSpec((size, LANES), lambda i, *_: (i, 0))] * n_tp,
        ),
        out_shape=[
            jax.ShapeDtypeStruct((some * groups, width), BF16),
            jax.ShapeDtypeStruct((rows, width), BF16),
            jax.ShapeDtypeStruct((heads, rows, 3 * HEAD_V), BF16),
        ]
        + [jax.ShapeDtypeStruct((some * size, LANES), BF16)] * n_tp,
        cost_estimate=pl.CostEstimate(
            flops=2 * rows * width * (cols + length) + 4 * heads * rows * length * HEAD_V,
            bytes_accessed=2 * (rows * width * 2 + rows * cols * 2 + width * cols),
            transcendentals=heads * rows * length,
        ),
        name="forward",
    )(ids, counts, x, gain, weight)


def place_kernel(columns, index_ref, *refs):
    out_refs = refs[-columns:]
    data = jnp.concatenate([ref[...] for ref in refs[:-columns]], axis=0)
    count = data.shape[0]
    axis = 0 if index_ref.shape[0] == 1 else 1
    out = mm(one_hot(iota((count, count), axis) == index_ref[...]), data).astype(BF16)
    size = count // columns
    for part in range(columns):
        out_refs[part][...] = out[part * size : (part + 1) * size]


def place(index, parts, columns, name):
    count = sum(part.shape[0] for part in parts)
    width = parts[0].shape[1]
    return pl.pallas_call(
        functools.partial(place_kernel, columns),
        out_shape=[jax.ShapeDtypeStruct((count // columns, width), BF16)] * columns,
        cost_estimate=pl.CostEstimate(
            flops=2 * count * count * width, bytes_accessed=4 * count * width, transcendentals=0
        ),
        name=name,
    )(index, *parts)


def merge_kernel(n_tp, n_parts, n_came, depth, ids, counts, *refs):
    refs = list(refs)
    head_refs = [[refs.pop(0) for _ in range(n_tp)] for _ in range(n_parts)]
    own_refs = [refs.pop(0) for _ in range(n_parts)]
    w_ref, wg_ref, wp_ref, gain_ref, send_ref, back_ref = (refs.pop(0) for _ in range(6))
    came = [refs.pop(0) for _ in range(n_came)]
    keep_ref, away_ref, grad_ref = (refs.pop(0) for _ in range(3))
    gh_refs = [refs.pop(0) for _ in range(n_tp)]
    head_out_refs = [refs.pop(0) for _ in range(n_tp)]
    (weights,) = refs
    rows = grad_ref.shape[0]
    images = counts.shape[0]
    groups = rows // images
    size = packed_rows(groups, depth)
    grp = ids[1]
    half = wg_ref.shape[1]
    for step in range(n_tp - 1):
        weights[step, pl.ds(pl.multiple_of(grp * half, half), half)] = wg_ref[step]
        weights[step, pl.ds(pl.multiple_of((1 - grp) * half, half), half)] = wp_ref[step]
    residual = jnp.concatenate([ref[...] for ref in own_refs], axis=0).astype(F32)
    for step in range(n_tp):
        parts = []
        for part in range(n_parts):
            for image in range(images // n_parts):
                parts.append(unpack(head_refs[part][step][image * size : (image + 1) * size], groups, depth))
        mine = jnp.concatenate(parts, axis=0)
        head_out_refs[step][...] = mine
        residual += mm(mine, weights[step - 1] if step else w_ref[...])
    group = iota((rows, 1), 0)
    live = jnp.zeros((rows, 1), F32)
    for image in range(images):
        inside = (group >= image * groups) & ((group - image * groups) * n_tp < counts[image])
        inside = inside & (group < (image + 1) * groups)
        live = jnp.where(inside, 1.0, live)
    gain = gain_ref[...]
    center = residual - jnp.mean(residual, axis=-1, keepdims=True)
    spread = jnp.mean(center * center, axis=-1, keepdims=True)
    inv = lax.rsqrt(spread + 1e-06)
    unit = center * inv
    incoming = mm(
        one_hot(iota((rows, rows), 1) == back_ref[...]), jnp.concatenate([ref[...] for ref in came], axis=0)
    )
    scaled = incoming * live * gain
    grad = inv * (
        scaled
        - jnp.mean(scaled, axis=-1, keepdims=True)
        - unit * jnp.mean(scaled * unit, axis=-1, keepdims=True)
    )
    grad = grad.astype(BF16)
    grad_ref[...] = grad
    for step in range(n_tp):
        out = mm(grad, weights[step - 1] if step else w_ref[...], NT)
        for image in range(images):
            gh_refs[step][image * size : (image + 1) * size] = pack(
                out[image * groups : (image + 1) * groups]
            ).astype(BF16)
    merged = (unit * gain * live).astype(BF16)
    outgoing = mm(one_hot(iota((rows, rows), 0) == send_ref[...]), merged).astype(BF16)
    keep_ref[...] = outgoing[: rows // 2]
    away_ref[...] = outgoing[rows // 2 :]


def merge(ids, counts, heads, owns, weight, w_got, w_partner, gain, send_row, back_col, came):
    n_tp = len(heads[0])
    width = weight.shape[1]
    rows = sum(own.shape[0] for own in owns)
    depth = weight.shape[0]
    args = [*sum(heads, []), *owns, weight, w_got, w_partner, gain, send_row, back_col, *came]
    size = sum(part[0].shape[0] for part in heads)
    out_shape = (
        [jax.ShapeDtypeStruct((rows // 2, width), BF16)] * 2
        + [jax.ShapeDtypeStruct((rows, width), BF16)]
        + [jax.ShapeDtypeStruct((size, LANES), BF16)] * n_tp
        + [jax.ShapeDtypeStruct((rows, depth), BF16)] * n_tp
    )
    return pl.pallas_call(
        functools.partial(merge_kernel, n_tp, len(heads), len(came), depth),
        grid_spec=pltpu.PrefetchScalarGridSpec(
            num_scalar_prefetch=2,
            grid=(1,),
            in_specs=[whole(arg) for arg in args],
            out_specs=[whole(out) for out in out_shape],
            scratch_shapes=[pltpu.VMEM((n_tp - 1, depth, width), BF16)],
        ),
        out_shape=out_shape,
        cost_estimate=pl.CostEstimate(
            flops=4 * rows * width * depth * n_tp + 4 * rows * rows * width,
            bytes_accessed=2 * (n_tp * depth * width + 6 * rows * width),
            transcendentals=rows,
        ),
        name="merge",
    )(ids, counts, *args)


def outer_kernel(n_tp, ids, g_ref, *refs):
    heads, keep_refs, away_ref = refs[:n_tp], refs[n_tp : 2 * n_tp], refs[2 * n_tp]
    half = g_ref.shape[1] // 2
    near = g_ref[:, pl.ds(pl.multiple_of(ids[1] * half, half), half)]
    far = g_ref[:, pl.ds(pl.multiple_of((1 - ids[1]) * half, half), half)]
    for step in range(n_tp):
        mine = heads[step][...]
        keep_refs[step][...] = mm(mine, near, TN).astype(BF16)
        away_ref[step] = mm(mine, far, TN).astype(BF16)


def outer(ids, grad, heads):
    rows, width = grad.shape
    n_tp = len(heads)
    depth = heads[0].shape[1]
    args = [grad, *heads]
    out_shape = [jax.ShapeDtypeStruct((depth, width // 2), BF16)] * n_tp
    out_shape = out_shape + [jax.ShapeDtypeStruct((n_tp, depth, width // 2), BF16)]
    return pl.pallas_call(
        functools.partial(outer_kernel, n_tp),
        grid_spec=pltpu.PrefetchScalarGridSpec(
            num_scalar_prefetch=1,
            grid=(1,),
            in_specs=[whole(arg) for arg in args],
            out_specs=[whole(out) for out in out_shape],
        ),
        out_shape=out_shape,
        cost_estimate=pl.CostEstimate(
            flops=2 * rows * width * depth * n_tp,
            bytes_accessed=2 * (rows * width + n_tp * depth * (rows + width)),
            transcendentals=0,
        ),
        name="outer",
    )(ids, *args)


def backward_kernel(n_tp, n_parts, first, depth, ids, counts, *refs):
    refs = list(refs)
    qkv_refs = [refs.pop(0) for _ in range(n_parts)]
    normed_refs = [refs.pop(0) for _ in range(n_parts)]
    g_refs = [refs.pop(0) for _ in range(n_tp)]
    keep_ref, away_ref, cols_ref = refs
    images = counts.shape[0]
    heads = qkv_refs[0].shape[0]
    each = images // n_parts
    rows = qkv_refs[0].shape[1]
    length = rows // each
    groups = length // n_tp
    size = packed_rows(groups, depth)
    for part in range(n_parts):

        def one(image, carry, part=part):
            base = pl.multiple_of(image * length, length)
            spot = pl.multiple_of((image + part * each) * size, size)
            live = (iota((length, 1), 0) % groups) * n_tp < counts[image + part * each]
            g_all = jnp.concatenate([unpack(ref[pl.ds(spot, size), :], groups, depth) for ref in g_refs], axis=0)
            outs = []
            for head in range(heads):
                lane = (first + head) * HEAD_V
                mine = qkv_refs[part][head, pl.ds(base, length), :]
                q, k, v = (mine[:, i * HEAD_V : (i + 1) * HEAD_V] for i in range(3))
                g = g_all[:, lane : lane + HEAD_V]
                scores = jnp.where(live, mm(k, q, NT) * HEAD_V ** (-0.5), -1e30)
                scores = jnp.exp(scores - jnp.max(scores, axis=0, keepdims=True))
                probs = scores * (1.0 / jnp.sum(scores, axis=0, keepdims=True))
                grad_probs = mm(v, g, NT).astype(BF16).astype(F32)
                delta = jnp.sum(probs * grad_probs, axis=0, keepdims=True)
                grad_scores = (probs * (grad_probs - delta) * HEAD_V ** (-0.5)).astype(BF16)
                outs.append(mm(k.T, grad_scores))
                outs.append(mm(q.T, grad_scores, NT))
                outs.append(mm(g.T, probs.astype(BF16), NT))
            at = pl.multiple_of((image + part * each) * length, length)
            cols_ref[:, pl.ds(at, length)] = jnp.concatenate(outs, axis=0).astype(BF16)
            return carry

        lax.fori_loop(0, each, one, 0)
    half = normed_refs[0].shape[1] // 2
    for away, ref in enumerate((keep_ref, away_ref)):
        lane = pl.ds(pl.multiple_of((ids[1] ^ away) * half, half), half)
        value = mm(cols_ref[:, :rows], normed_refs[0][:, lane])
        for part in range(1, n_parts):
            value += mm(cols_ref[:, part * rows : (part + 1) * rows], normed_refs[part][:, lane])
        ref[...] = value.astype(ref.dtype)


def backward(ids, counts, qkv, normed, grads, first, heads, depth):
    n_tp = len(grads)
    n_parts = len(qkv)
    _, rows, cols = qkv[0].shape
    width = normed[0].shape[1]
    total = rows * n_parts
    length = total // counts.shape[0]
    args = [*normed, *grads]
    out_shape = [
        jax.ShapeDtypeStruct((heads * cols, width // 2), F32),
        jax.ShapeDtypeStruct((heads * cols, width // 2), BF16),
    ]
    return pl.pallas_call(
        functools.partial(backward_kernel, n_tp, n_parts, first, depth),
        grid_spec=pltpu.PrefetchScalarGridSpec(
            num_scalar_prefetch=2,
            grid=(1,),
            in_specs=[pl.BlockSpec((heads, rows, cols), lambda i, *_: (first // heads, 0, 0))] * n_parts
            + [whole(arg) for arg in args],
            out_specs=[whole(out) for out in out_shape],
            scratch_shapes=[pltpu.VMEM((heads * cols, total), BF16)],
        ),
        out_shape=out_shape,
        cost_estimate=pl.CostEstimate(
            flops=2 * total * width * heads * cols + 10 * heads * total * length * HEAD_V,
            bytes_accessed=2 * (total * width + 2 * total * heads * cols + 2 * width * heads * cols),
            transcendentals=heads * total * length,
        ),
        name="backward",
    )(ids, counts, *qkv, *args)


def fold_kernel(n_in, n_seq, ids, *refs):
    in_refs, out_refs, parts = refs[:n_in], refs[n_in:-1], refs[-1]
    total = in_refs[0][...].astype(F32)
    for ref in in_refs[1:]:
        total += ref[...].astype(F32)
    chunk = total.shape[1] // n_seq
    for part in range(n_seq):
        parts[part] = pack(total[:, part * chunk : (part + 1) * chunk]).astype(BF16)
    for step in range(n_seq):
        out_refs[step][...] = parts[ids[2] ^ step]


def fold(ids, terms, n_seq):
    rows, cols = terms[0].shape
    size = packed_rows(rows, cols // n_seq)
    out_shape = [jax.ShapeDtypeStruct((size, LANES), BF16)] * n_seq
    return pl.pallas_call(
        functools.partial(fold_kernel, len(terms), n_seq),
        grid_spec=pltpu.PrefetchScalarGridSpec(
            num_scalar_prefetch=1,
            grid=(1,),
            in_specs=[whole(term) for term in terms],
            out_specs=[whole(out) for out in out_shape],
            scratch_shapes=[pltpu.VMEM((n_seq, size, LANES), BF16)],
        ),
        out_shape=out_shape,
        cost_estimate=pl.CostEstimate(
            flops=rows * cols * len(terms), bytes_accessed=4 * rows * cols * len(terms), transcendentals=0
        ),
        name="fold",
    )(ids, *terms)


def finish_kernel(n_seq, shapes, *refs):
    out_ref = refs[-1]
    pieces = []
    for piece, (rows, cols) in enumerate(shapes):
        mine = refs[piece * n_seq : (piece + 1) * n_seq]
        total = mine[0][...].astype(F32)
        for ref in mine[1:]:
            total += ref[...].astype(F32)
        pieces.append(unpack(total, rows, cols).T)
    out_ref[...] = jnp.concatenate(pieces, axis=1)


def finish(pieces, shapes, name):
    n_seq = len(pieces[0])
    cols = shapes[0][1]
    total = sum(rows for rows, _ in shapes)
    return pl.pallas_call(
        functools.partial(finish_kernel, n_seq, shapes),
        out_shape=jax.ShapeDtypeStruct((cols, total), F32),
        cost_estimate=pl.CostEstimate(
            flops=cols * total * n_seq, bytes_accessed=(4 + 2 * n_seq) * cols * total, transcendentals=0
        ),
        name=name,
    )(*sum(pieces, []))


def exchange(parts, axes, size):
    return [parts[0]] + [swap(parts[s], axes, s, size) for s in range(1, size)]


def spread_out(kept, away, n_seq):
    got = swap(away, "grp", 1, 2)
    size = kept.shape[0] // n_seq
    cuts = [slice(step * size, (step + 1) * size) for step in range(n_seq)]
    parts = exchange([jnp.concatenate([kept[cut], got[cut]], axis=0) for cut in cuts], "seq", n_seq)
    if parts[0].ndim > 1 and size % 16:
        parts = [jnp.concatenate(parts, axis=0)]
    return parts


def shards(patches_in, gain_attn, gain_merge, qkv_weight, out_weight, cotangent, patch_counts, block_target):
    n_grp, n_seq, n_tp = (lax.axis_size(name) for name in ("grp", "seq", "tp"))
    grp, seq, tp = (lax.axis_index(name).astype(jnp.int32) for name in ("grp", "seq", "tp"))
    ids = jnp.stack([tp, grp, seq])
    rows, width = patches_in.shape
    images = patch_counts.shape[0]
    blocks = block_target.shape[0]
    block_rows = rows // n_tp // blocks
    per_peer = blocks // (n_grp * n_seq)
    depth = out_weight.shape[0]

    target = block_target // blocks
    slot = block_target % blocks
    away = (target // n_seq) ^ grp
    step = (target % n_seq) ^ seq
    key = away * n_seq + step
    index = jnp.arange(blocks, dtype=jnp.int32)
    earlier = (key[None, :] == key[:, None]) & (index[None, :] < index[:, None])
    rank = jnp.sum(earlier.astype(jnp.int32), axis=1)
    sent_at = key * per_peer + rank
    back_at = (step * n_grp + away) * per_peer + rank
    sent_slots = jnp.sum(jnp.where(sent_at[None, :] == index[:, None], slot[None, :], 0), axis=1)
    wide = jnp.arange(block_rows, dtype=jnp.int32)
    send_row = (sent_at[:, None] * block_rows + wide[None, :]).reshape(1, -1)
    back_col = (back_at[:, None] * block_rows + wide[None, :]).reshape(-1, 1)
    slot_parts = sent_slots.reshape(n_grp, n_seq * per_peer)
    got_slots = jnp.stack(spread_out(slot_parts[0], slot_parts[1], n_seq))
    got_slots = got_slots.reshape(n_seq, n_grp, per_peer)
    slot_row = got_slots.reshape(-1, 1) * block_rows + wide[None, :]
    place_row = slot_row.reshape(1, -1)
    return_col = got_slots.transpose(1, 0, 2).reshape(-1, 1) * block_rows + wide[None, :]
    return_col = return_col.reshape(-1, 1)

    half = depth // n_grp
    w_half = lax.dynamic_slice_in_dim(out_weight, grp * half, half, 0)
    w_got = jnp.stack([swap(w_half, "tp", s, n_tp) for s in range(1, n_tp)])
    w_partner = swap(w_got, "grp", 1, n_grp)

    turned_weight = qkv_weight.T
    n_parts = 2 if images % 2 == 0 else 1
    owns, normed, qkv, heads = [], [], [], []
    for part in range(n_parts):
        own, norm, proj, *head = forward(
            ids, patch_counts, patches_in, gain_attn[None], turned_weight, n_tp, part * images // n_parts, images // n_parts
        )
        owns.append(own)
        normed.append(norm)
        qkv.append(proj)
        if part == 0:
            kept, gone = place(return_col, [cotangent], n_grp, "returning")
            kept, gone, patches_in = lax.optimization_barrier((kept, gone, patches_in))
        heads.append(exchange(head, "tp", n_tp))
    came = spread_out(kept, gone, n_seq)

    kept, gone, grad_own, *rest = merge(
        ids, patch_counts, heads, owns, out_weight, w_got, w_partner, gain_merge[None], send_row, back_col, came
    )
    grads = exchange(rest[:n_tp], "tp", n_tp)
    arrived = spread_out(kept, gone, n_seq)

    *near, far = outer(ids, grad_own, rest[n_tp:])
    far = swap(far, "grp", 1, n_grp)
    near = [(near[s].astype(F32) + far[s].astype(F32)).astype(BF16) for s in range(n_tp)]
    terms = exchange(near, "tp", n_tp)
    out_parts = exchange(fold(ids, terms, n_seq), "seq", n_seq)
    grad_out = finish([out_parts], [(depth, width // n_grp // n_seq)], "finish_out").T

    per_call = 2
    pieces, shapes = [], []
    for first in range(0, qkv[0].shape[0], per_call):
        kept, gone = backward(ids, patch_counts, qkv, normed, grads, first, per_call, depth)
        parts = fold(ids, [kept, swap(gone, "grp", 1, n_grp)], n_seq)
        pieces.append(exchange(parts, "seq", n_seq))
        shapes.append((kept.shape[0], width // n_grp // n_seq))
    grad_qkv = finish(pieces, shapes, "finish_qkv")
    (image_rows,) = place(place_row, arrived, 1, "placing")
    return (image_rows, grad_qkv, grad_out)


def solution(mesh):
    return jax.shard_map(
        shards,
        mesh=mesh,
        in_specs=(
            P(("grp", "seq"), None),
            P(),
            P(),
            P(None, "tp"),
            P("tp", None),
            P(("grp", "seq"), "tp"),
            P(("grp", "seq")),
            P(("grp", "seq")),
        ),
        out_specs=(P(("grp", "seq"), "tp"), P(("grp", "seq"), "tp"), P("tp", ("grp", "seq"))),
        check_vma=False,
    )
```
